32 devices in a mesh: section: 2 (over core), dp: 16 (over z, y, x).
Axes of the slice: x: 2, y: 2, z: 4, core: 2. Of those that a mesh axis runs over, the one named last changes fastest.
Arguments:
- inputs: bfloat16 [2, 16, 320, 128], P(None, 'dp'), may hold values from -6 to 6
- out_grad: bfloat16 [2, 16, 320, 128], P(None, 'dp'), may hold values from -0.09375 to 0.09375
- weights: bfloat16 [2, 320, 9, 320], P('section'), may hold values from -0.078125 to 0.078125
- momentum: float32 [2, 320, 9, 320], P('section'), may hold values from -6 to 6
Outputs:
- new_weights: bfloat16 [2, 320, 9, 320], P('section')
- new_momentum: float32 [2, 320, 9, 320], P('section')
The draws below stay inside these ranges and needn't reach their ends.
All inputs are finite; a program needn't handle non-finite values.
Results may differ from the reference program's by a relative error of at most 0.02.
Values may be sent and summed in bfloat16 or wider, within the bound.
A program may use at most 128 MiB of HBM per device.

```python
import jax
import jax.numpy as jnp

C = 320
TILE_H = 8
TILE_W = 16
TILE = 128
BATCH = 16
LAYERS = 2


def block_scale(stream_key, dims, split, smallest, high):
    def one(dim, shards_of):
        steps = jax.random.uniform(jax.random.fold_in(jax.random.fold_in(stream_key, 6), dim), (shards_of,), jnp.float32, smallest / len(split), high / len(split))
        return jnp.repeat(jnp.exp(steps), dims[dim] // shards_of).reshape((-1,) + (1,) * (len(dims) - dim - 1))

    factor_of = one(*split[0])
    for cut in split[1:]:
        factor_of = factor_of * one(*cut)
    return factor_of


def gaussian(stream_key, extent, scale, bound, cuts=(), kind=jnp.bfloat16):
    entries = scale * jax.random.normal(stream_key, extent, jnp.float32)
    if cuts:
        entries = entries * block_scale(stream_key, extent, cuts, -0.22, 0.18)
    return jnp.clip(entries, -bound, bound).astype(kind)


def setup_inputs(seed: int = 0) -> dict:
    seeds = jax.random.split(jax.random.key(seed), 5)
    inputs = gaussian(seeds[0], (2, BATCH, C, TILE), 1.0, 6.0, ((1, 16),))
    out_grad = gaussian(seeds[1], (2, BATCH, C, TILE), ((2 * BATCH * TILE) ** -0.5), 0.09375, ((1, 16),))
    weights = gaussian(seeds[2], (LAYERS, C, 9, C), (18 * C) ** -0.5, 0.078125, ((0, 2),))
    momentum = gaussian(seeds[3], (LAYERS, C, 9, C), 1.0, 6.0, ((0, 2),), jnp.float32)
    return dict(inputs=inputs, out_grad=out_grad, weights=weights, momentum=momentum)


momentum_rate = 0.9
learn_rate = 0.02


def expand(active):
    dims_in = active.shape
    grid_view = active.reshape(dims_in[:-1] + (TILE_H, TILE_W))
    padding = [(0, 0)] * (grid_view.ndim - 2) + [(1, 1), (1, 1)]
    padded = jnp.pad(grid_view, padding)
    pieces = [padded[..., row_off:row_off + TILE_H, col_off:col_off + TILE_W] for row_off in range(3) for col_off in range(3)]
    stacked = jnp.stack(pieces, axis=-4)
    return stacked.reshape(dims_in[:-2] + (9 * dims_in[-2], dims_in[-1]))


def fold(spread):
    dims_in = spread.shape
    channels = dims_in[-2] // 9
    pieces = spread.reshape(dims_in[:-2] + (9, channels, TILE_H, TILE_W))
    summed = jnp.zeros(dims_in[:-2] + (channels, TILE_H + 2, TILE_W + 2), spread.dtype)
    leading = [(0, 0)] * (len(dims_in) - 1)
    for row_off in range(3):
        for col_off in range(3):
            padding = leading + [(row_off, 2 - row_off), (col_off, 2 - col_off)]
            summed = summed + jnp.pad(pieces[..., 3 * row_off + col_off, :, :, :], padding)
    return summed[..., 1:-1, 1:-1].reshape(dims_in[:-2] + (channels, dims_in[-1]))


def activate(hidden):
    return jax.nn.silu(hidden.astype(jnp.float32)).astype(jnp.bfloat16)


def slope(hidden):
    value = hidden.astype(jnp.float32)
    sig = jax.nn.sigmoid(value)
    return sig * (1.0 + value * (1.0 - sig))


def reference(inputs, out_grad, weights, momentum):
    channels = weights.shape[1]
    layer_count = weights.shape[0]
    flat_w = weights.reshape(layer_count, channels, 9 * channels)
    hidden = inputs.reshape((-1, channels, inputs.shape[-1]))
    saved = []
    for layer_num in range(layer_count):
        saved.append(hidden)
        columns = expand(activate(hidden))
        conv_out = jnp.einsum('ok,nkp->nop', flat_w[layer_num].astype(jnp.float32), columns.astype(jnp.float32))
        hidden = (hidden.astype(jnp.float32) + conv_out).astype(jnp.bfloat16)
    cotangent = out_grad.reshape((-1, channels, out_grad.shape[-1]))
    grads = []
    for layer_num in range(layer_count - 1, -1, -1):
        stored = saved[layer_num]
        columns = expand(activate(stored))
        grads.insert(0, jnp.einsum('nop,nkp->ok', cotangent.astype(jnp.float32), columns.astype(jnp.float32)))
        spread = jnp.einsum('ok,nop->nkp', flat_w[layer_num].astype(jnp.float32), cotangent.astype(jnp.float32))
        backward = fold(spread)
        cotangent = (cotangent.astype(jnp.float32) + slope(stored) * backward).astype(jnp.bfloat16)
    summed = jnp.stack(grads).reshape(weights.shape)
    new_momentum = momentum_rate * momentum + summed
    new_weights = (weights.astype(jnp.float32) - learn_rate * new_momentum).astype(jnp.bfloat16)
    return new_weights, new_momentum
```

```python
import jax
import jax.numpy as jnp
from jax import lax
from jax.sharding import PartitionSpec as P

TILE_H = 8
TILE_W = 16
momentum_rate = 0.9
learn_rate = 0.02


def shifted(value, row_off, col_off):
    lane = lax.broadcasted_iota(jnp.int32, value.shape, value.ndim - 1)
    row = lane // TILE_W + row_off
    col = lane % TILE_W + col_off
    good = (row >= 0) & (row < TILE_H) & (col >= 0) & (col < TILE_W)
    moved = jnp.roll(value, -(row_off * TILE_W + col_off), axis=-1)
    return jnp.where(good, moved, jnp.zeros_like(moved))


OFFS = [(i, j) for i in (-1, 0, 1) for j in (-1, 0, 1)]


def activate(hidden):
    return jax.nn.silu(hidden.astype(jnp.float32)).astype(jnp.bfloat16)


def slope(hidden):
    value = hidden.astype(jnp.float32)
    sig = jax.nn.sigmoid(value)
    return sig * (1.0 + value * (1.0 - sig))


def dot(a, b, dims):
    return lax.dot_general(a, b, (dims, ((), ())), preferred_element_type=jnp.float32)


def shards(inputs, out_grad, weights, momentum):
    sections = lax.axis_size("section")
    position = lax.axis_index("section")
    channels = weights.shape[1]
    taps = jnp.transpose(weights[0], (1, 0, 2))
    tiles = inputs.reshape((-1,) + inputs.shape[2:])
    targets = out_grad.reshape((-1,) + inputs.shape[2:])
    hidden = tiles
    for step in range(sections - 1):
        act = activate(hidden)
        conv = sum(
            jnp.einsum("oc,ncp->nop", taps[k], shifted(act, *off), preferred_element_type=jnp.float32)
            for k, off in enumerate(OFFS)
        )
        out = (hidden.astype(jnp.float32) + conv).astype(jnp.bfloat16)
        moved = lax.ppermute(out, "section", [(i, i + 1) for i in range(sections - 1)])
        hidden = jnp.where(position == step + 1, moved, hidden)
    grad_out = targets
    for step in range(sections - 1):
        back = sum(
            shifted(
                jnp.einsum("oc,nop->ncp", taps[k], grad_out, preferred_element_type=jnp.float32),
                -off[0],
                -off[1],
            )
            for k, off in enumerate(OFFS)
        )
        out = (grad_out.astype(jnp.float32) + slope(hidden) * back).astype(jnp.bfloat16)
        moved = lax.ppermute(out, "section", [(i + 1, i) for i in range(sections - 1)])
        grad_out = jnp.where(position == sections - 2 - step, moved, grad_out)
    act = activate(hidden)
    grads = [
        jnp.einsum("nop,ncp->oc", grad_out, shifted(act, *off), preferred_element_type=jnp.float32)
        for off in OFFS
    ]
    local = jnp.stack(grads, axis=0).astype(jnp.bfloat16)
    summed = lax.psum(local, "dp").astype(jnp.float32)
    summed = jnp.transpose(summed, (1, 0, 2))[None]
    new_momentum = momentum_rate * momentum + summed
    new_weights = (weights.astype(jnp.float32) - learn_rate * new_momentum).astype(jnp.bfloat16)
    return (new_weights, new_momentum)


def solution(mesh):
    in_specs = (
        P(None, "dp", None, None),
        P(None, "dp", None, None),
        P("section", None, None, None),
        P("section", None, None, None),
    )
    out_specs = (P("section", None, None, None), P("section", None, None, None))
    return jax.shard_map(shards, mesh=mesh, in_specs=in_specs, out_specs=out_specs, check_vma=False)
```

```python
import functools

import jax
import jax.numpy as jnp
from jax import lax
from jax.experimental import pallas as pl
from jax.experimental.pallas import tpu as pltpu
from jax.sharding import PartitionSpec as P

TILE_H = 8
TILE_W = 16
momentum_rate = 0.9
learn_rate = 0.02
MESH = pl.DeviceIdType.MESH
OFFS = [(i, j) for i in (-1, 0, 1) for j in (-1, 0, 1)]
TAPS = 9
PLANE = 4


def masks_of(pixels):
    lane = lax.broadcasted_iota(jnp.int32, (1, pixels), 1)
    out = {}
    for off in OFFS:
        row = lane // TILE_W + off[0]
        col = lane % TILE_W + off[1]
        good = (row >= 0) & (row < TILE_H) & (col >= 0) & (col < TILE_W)
        out[off] = jnp.where(good, 1.0, 0.0)
    return out


def shifted(value, off, masks):
    if off == (0, 0):
        return value
    steps = -(off[0] * TILE_W + off[1]) % value.shape[-1]
    return pltpu.roll(value, steps, axis=1) * masks[off]


def dot(a, b, dims):
    return lax.dot_general(a, b, (dims, ((), ())), preferred_element_type=jnp.float32)


def act_of(hidden):
    value = hidden.astype(jnp.float32)
    return (value * jax.nn.sigmoid(value)).astype(jnp.bfloat16)


def step_kernel(
    sections, count, units,
    x_ref, y_ref, w_ref, out_ref,
    hin, gin, hout, gout, back, held_h, held_g, acc, send_part, got_part, gathered,
    line_send, line_recv, h_send, h_recv, g_send, g_recv,
    part_send, part_recv, z_send, all_recv, near_send, far_send, out_sem,
):
    groups = count // PLANE
    pos = lax.axis_index("section")
    me = lax.axis_index("dp")
    quarter = lax.rem(me, PLANE)
    group = lax.div(me, PLANE)
    first = pos == 0
    last = pos == sections - 1
    tiles, channels, pixels = x_ref.shape
    rows = channels // PLANE
    chunk = units * 16
    masks = masks_of(pixels)

    def mate(j):
        other = jnp.bitwise_xor(quarter, j)
        return other, (pos, group * PLANE + other)

    def column(i):
        other = lax.rem(group + i, groups)
        return other, (pos, other * PLANE + quarter)

    barrier = pltpu.get_barrier_semaphore()

    def greet(device):
        pl.semaphore_signal(barrier, inc=1, device_id=device, device_id_type=MESH)

    for j in range(1, PLANE):
        greet(mate(j)[1])
    for i in range(1, groups):
        greet(column(i)[1])

    @pl.when(jnp.logical_not(first))
    def _():
        greet((pos - 1, me))

    @pl.when(jnp.logical_not(last))
    def _():
        greet((pos + 1, me))

    ends = jnp.where(first, 0, 1) + jnp.where(last, 0, 1)
    pl.semaphore_wait(barrier, PLANE - 1 + groups - 1 + ends)

    def copy(src, dst, send_sem, recv_sem, device):
        return pltpu.make_async_remote_copy(
            src_ref=src, dst_ref=dst, send_sem=send_sem, recv_sem=recv_sem,
            device_id=device, device_id_type=MESH,
        )

    def h_copy(src, j):
        return copy(src, held_h.at[quarter], h_send.at[j], h_recv.at[quarter], mate(j)[1])

    def g_copy(src, j):
        other, device = mate(j)
        start = pl.multiple_of(other * rows, 16)
        return copy(
            src.at[:, pl.ds(start, rows), :], held_g.at[quarter], g_send.at[j], g_recv.at[quarter], device
        )

    def h_spread(src):
        for j in range(1, PLANE):
            h_copy(src, j).start()

    def g_spread(src):
        for j in range(1, PLANE):
            g_copy(src, j).start()

    def h_line():
        return copy(hout, hin, line_send.at[0], line_recv.at[0], (pos + 1, me))

    def g_line():
        return copy(gout, gin, line_send.at[1], line_recv.at[1], (pos - 1, me))

    def find_back():
        total = None
        values = [gin[t].astype(jnp.float32) for t in range(tiles)]
        for k, off in enumerate(OFFS):
            flip = (-off[0], -off[1])
            moved = [shifted(v, flip, masks).astype(jnp.bfloat16) for v in values]
            term = dot(w_ref[k], jnp.concatenate(moved, axis=1), ((0,), (0,)))
            total = term if total is None else total + term
        for t in range(tiles):
            back[t] = total[:, t * pixels : (t + 1) * pixels]

    @pl.when(first)
    def _():
        h_spread(x_ref)
        hin[...] = x_ref[...]

    @pl.when(last)
    def _():
        g_spread(y_ref)
        gin[...] = y_ref[...]

    if sections > 1:

        @pl.when(last)
        def _():
            find_back()

        @pl.when(jnp.logical_not(first))
        def _():
            copy(hout, hin, line_send.at[0], line_recv.at[0], (pos - 1, me)).wait_recv()
            h_spread(hin)

        @pl.when(jnp.logical_not(last))
        def _():
            values = [act_of(hin[t]).astype(jnp.float32) for t in range(tiles)]
            total = None
            for k, off in enumerate(OFFS):
                moved = [shifted(v, off, masks).astype(jnp.bfloat16) for v in values]
                term = dot(w_ref[k], jnp.concatenate(moved, axis=1), ((1,), (0,)))
                total = term if total is None else total + term
            for t in range(tiles):
                piece = total[:, t * pixels : (t + 1) * pixels]
                hout[t] = (hin[t].astype(jnp.float32) + piece).astype(jnp.bfloat16)
            h_line().start()
            copy(gout, gin, line_send.at[1], line_recv.at[1], (pos + 1, me)).wait_recv()
            g_spread(gin)

        if sections > 2:

            @pl.when(jnp.logical_not(first) & jnp.logical_not(last))
            def _():
                find_back()

        @pl.when(jnp.logical_not(first))
        def _():
            for t in range(tiles):
                value = hin[t].astype(jnp.float32)
                sig = jax.nn.sigmoid(value)
                slope = sig * (1.0 + value * (1.0 - sig))
                gout[t] = (gin[t].astype(jnp.float32) + slope * back[t]).astype(jnp.bfloat16)
            g_line().start()

    def gradient(h_of, g_of):
        acts = jnp.concatenate([act_of(h_of(t)) for t in range(tiles)], axis=1)
        values = [g_of(t).astype(jnp.float32) for t in range(tiles)]
        stacked = []
        for off in OFFS:
            flip = (-off[0], -off[1])
            moved = [shifted(v, flip, masks).astype(jnp.bfloat16) for v in values]
            stacked.append(jnp.concatenate(moved, axis=1))
        return dot(jnp.concatenate(stacked, axis=0), acts, ((1,), (1,)))

    full = TAPS * rows
    mine = pl.multiple_of(quarter * rows, 16)
    acc[0:full, :] = gradient(lambda t: hin[t], lambda t: gin[t, pl.ds(mine, rows), :])
    if groups * chunk > full:
        acc[full:, :] = jnp.zeros((groups * chunk - full, channels), jnp.float32)
    for j in range(1, PLANE):
        other, device = mate(j)
        copy(held_h.at[other], held_h.at[other], h_send.at[j], h_recv.at[other], device).wait_recv()
        copy(held_g.at[other], held_g.at[other], g_send.at[j], g_recv.at[other], device).wait_recv()
        acc[0:full, :] += gradient(lambda t: held_h[other, t], lambda t: held_g[other, t])

    send_part[...] = acc[...].astype(jnp.bfloat16)

    def span(index):
        return pl.ds(pl.multiple_of(index * chunk, 16), chunk)

    def part_copy(i):
        other, device = column(i)
        return copy(send_part.at[span(other), :], got_part.at[group], part_send.at[i], part_recv.at[group], device)

    for i in range(1, groups):
        part_copy(i).start()
    total = acc[span(group), :]
    for i in range(1, groups):
        other, device = column(i)
        copy(got_part.at[other], got_part.at[other], part_send.at[i], part_recv.at[other], device).wait_recv()
        total = total + got_part[other].astype(jnp.float32)
    gathered[quarter, span(group), :] = total.astype(jnp.bfloat16)

    def block(source, part):
        return gathered.at[source, span(part), :]

    def z_copy(i):
        ref = block(quarter, group)
        return copy(ref, ref, z_send.at[i], all_recv.at[quarter, group], column(i)[1])

    def plane_copy(source, i, send_sem, j):
        part = column(i)[0]
        ref = block(source, part)
        return copy(ref, ref, send_sem, all_recv.at[source, part], mate(j)[1])

    def near(i, j):
        return plane_copy(quarter, i, near_send.at[j - 1, i], j)

    def far(i):
        if i % 2 == 0:
            return plane_copy(mate(1)[0], i, far_send.at[i], 2)
        return plane_copy(mate(2)[0], i, far_send.at[i], 1)

    def arrive(source, i):
        part = column(i)[0]
        ref = block(source, part)
        copy(ref, ref, far_send.at[i], all_recv.at[source, part], mate(1)[1]).wait_recv()

    for i in range(1, groups):
        z_copy(i).start()

    def relay(i):
        arrive(mate(1 if i % 2 == 0 else 2)[0], i)
        far(i).start()

    for i in range(groups):
        if i > 0:
            arrive(quarter, i)
        near(i, 1).start()
        near(i, 2).start()
        if i > 0:
            relay(i - 1)
    relay(groups - 1)
    for i in range(groups):
        arrive(mate(2 if i % 2 == 0 else 1)[0], i)
        arrive(mate(3)[0], i)

    result = pltpu.make_async_copy(gathered, out_ref, out_sem)
    result.start()
    for j in range(1, PLANE):
        h_copy(hin, j).wait_send()
        g_copy(gin, j).wait_send()
    for i in range(1, groups):
        part_copy(i).wait_send()
        z_copy(i).wait_send()
    for i in range(groups):
        near(i, 1).wait_send()
        near(i, 2).wait_send()
        far(i).wait_send()
    if sections > 1:

        @pl.when(jnp.logical_not(last))
        def _():
            h_line().wait_send()

        @pl.when(jnp.logical_not(first))
        def _():
            g_line().wait_send()

    result.wait()


def update_kernel(g_ref, w_ref, m_ref, new_w_ref, new_m_ref):
    quarters, rows, channels = g_ref.shape
    grad = g_ref[...].astype(jnp.float32).reshape(quarters * rows, channels)
    new_m = momentum_rate * m_ref[0] + grad
    new_m_ref[0] = new_m
    new_w_ref[0] = (w_ref[0].astype(jnp.float32) - learn_rate * new_m).astype(jnp.bfloat16)


def shards(sections, count, inputs, out_grad, weights, momentum):
    channels, pixels = inputs.shape[2:]
    x = inputs.reshape((-1, channels, pixels))
    y = out_grad.reshape((-1, channels, pixels))
    tiles = x.shape[0]
    w = jnp.transpose(weights[0], (1, 0, 2))
    m = jnp.transpose(momentum[0], (1, 0, 2))
    groups = count // PLANE
    rows = channels // PLANE
    units = -(-(TAPS * rows // 16) // groups)
    chunk = units * 16
    height = groups * chunk
    bf16, f32 = jnp.bfloat16, jnp.float32
    vmem = pl.BlockSpec(memory_space=pltpu.VMEM)
    dma = pltpu.SemaphoreType.DMA
    grads = pl.pallas_call(
        functools.partial(step_kernel, sections, count, units),
        out_shape=jax.ShapeDtypeStruct((PLANE, height, channels), bf16),
        in_specs=[vmem] * 3,
        out_specs=pl.BlockSpec(memory_space=pl.ANY),
        scratch_shapes=[
            pltpu.VMEM((tiles, channels, pixels), bf16),
            pltpu.VMEM((tiles, channels, pixels), bf16),
            pltpu.VMEM((tiles, channels, pixels), bf16),
            pltpu.VMEM((tiles, channels, pixels), bf16),
            pltpu.VMEM((tiles, channels, pixels), f32),
            pltpu.VMEM((PLANE, tiles, channels, pixels), bf16),
            pltpu.VMEM((PLANE, tiles, rows, pixels), bf16),
            pltpu.VMEM((height, channels), f32),
            pltpu.VMEM((height, channels), bf16),
            pltpu.VMEM((groups, chunk, channels), bf16),
            pltpu.VMEM((PLANE, height, channels), bf16),
            dma((2,)), dma((2,)), dma((PLANE,)), dma((PLANE,)), dma((PLANE,)), dma((PLANE,)),
            dma((groups,)), dma((groups,)), dma((groups,)), dma((PLANE, groups)),
            dma((2, groups)), dma((groups,)), dma(()),
        ],
        compiler_params=pltpu.CompilerParams(
            collective_id=0, has_side_effects=True, vmem_limit_bytes=48 * 1024 * 1024
        ),
    )(x, y, w)
    tap = lambda dtype: pl.BlockSpec((1, channels, channels), lambda k: (k, 0, 0))
    new_w, new_m = pl.pallas_call(
        update_kernel,
        grid=(TAPS,),
        out_shape=(
            jax.ShapeDtypeStruct((TAPS, channels, channels), bf16),
            jax.ShapeDtypeStruct((TAPS, channels, channels), f32),
        ),
        in_specs=[pl.BlockSpec((PLANE, rows, channels), lambda k: (0, k, 0)), tap(bf16), tap(f32)],
        out_specs=(tap(bf16), tap(f32)),
    )(grads, w, m)
    return jnp.transpose(new_w, (1, 0, 2))[None], jnp.transpose(new_m, (1, 0, 2))[None]


def solution(mesh):
    in_specs = (
        P(None, "dp", None, None),
        P(None, "dp", None, None),
        P("section", None, None, None),
        P("section", None, None, None),
    )
    out_specs = (P("section", None, None, None), P("section", None, None, None))
    body = functools.partial(shards, mesh.shape["section"], mesh.shape["dp"])
    return jax.shard_map(body, mesh=mesh, in_specs=in_specs, out_specs=out_specs, check_vma=False)
```

```python
import functools

import jax
import jax.numpy as jnp
from jax import lax
from jax.experimental import pallas as pl
from jax.experimental.pallas import tpu as pltpu
from jax.sharding import PartitionSpec as P

TILE_H = 8
TILE_W = 16
momentum_rate = 0.9
learn_rate = 0.02
MESH = pl.DeviceIdType.MESH
OFFS = [(i, j) for i in (-1, 0, 1) for j in (-1, 0, 1)]
TAPS = 9
PLANE = 4
LANES = 128


def masks_of(pixels):
    lane = lax.broadcasted_iota(jnp.int32, (1, pixels), 1)
    out = {}
    for off in OFFS:
        row = lane // TILE_W + off[0]
        col = lane % TILE_W + off[1]
        good = (row >= 0) & (row < TILE_H) & (col >= 0) & (col < TILE_W)
        out[off] = jnp.where(good, 1.0, 0.0)
    return out


def shifted(value, off, masks):
    if off == (0, 0):
        return value
    steps = -(off[0] * TILE_W + off[1]) % value.shape[-1]
    return pltpu.roll(value, steps, axis=1) * masks[off]


def dot(a, b, dims):
    return lax.dot_general(a, b, (dims, ((), ())), preferred_element_type=jnp.float32)


def act_of(hidden):
    value = hidden.astype(jnp.float32)
    return (value * jax.nn.sigmoid(value)).astype(jnp.bfloat16)


def step_kernel(
    sections, count, units,
    x_hbm, y_hbm, w_hbm, m_hbm, new_w_ref, new_m_ref,
    x_ref, y_ref, w_ref, hin, gin, hout, gout, back, held_h, held_g, acc, send_part, got_part, gathered,
    line_send, line_recv, h_send, h_recv, g_send, g_recv,
    part_send, part_recv, z_send, all_recv, near_send, far_send, load_sem,
):
    groups = count // PLANE
    pos = lax.axis_index("section")
    me = lax.axis_index("dp")
    quarter = lax.rem(me, PLANE)
    group = lax.div(me, PLANE)
    first = pos == 0
    last = pos == sections - 1
    tiles, channels, pixels = x_ref.shape
    loads = [
        pltpu.make_async_copy(src, dst, load_sem.at[n])
        for n, (src, dst) in enumerate(
            [(x_hbm, x_ref), (y_hbm, y_ref), (w_hbm, w_ref), (m_hbm, new_m_ref)]
        )
    ]
    for load in loads:
        load.start()
    rows = channels // PLANE
    chunk = units * 16
    masks = masks_of(pixels)

    def mate(j):
        other = jnp.bitwise_xor(quarter, j)
        return other, (pos, group * PLANE + other)

    def column(i):
        other = lax.rem(group + i, groups)
        return other, (pos, other * PLANE + quarter)

    barrier = pltpu.get_barrier_semaphore()

    def greet(device):
        pl.semaphore_signal(barrier, inc=1, device_id=device, device_id_type=MESH)

    for j in range(1, PLANE):
        greet(mate(j)[1])
    for i in range(1, groups):
        greet(column(i)[1])

    @pl.when(jnp.logical_not(first))
    def _():
        greet((pos - 1, me))

    @pl.when(jnp.logical_not(last))
    def _():
        greet((pos + 1, me))

    ends = jnp.where(first, 0, 1) + jnp.where(last, 0, 1)
    pl.semaphore_wait(barrier, PLANE - 1 + groups - 1 + ends)

    def copy(src, dst, send_sem, recv_sem, device):
        return pltpu.make_async_remote_copy(
            src_ref=src, dst_ref=dst, send_sem=send_sem, recv_sem=recv_sem,
            device_id=device, device_id_type=MESH,
        )

    def h_copy(src, j):
        return copy(src, held_h.at[quarter], h_send.at[j], h_recv.at[quarter], mate(j)[1])

    def g_copy(src, j):
        other, device = mate(j)
        start = pl.multiple_of(other * rows, 16)
        return copy(
            src.at[:, pl.ds(start, rows), :], held_g.at[quarter], g_send.at[j], g_recv.at[quarter], device
        )

    def h_spread(src):
        for j in range(1, PLANE):
            h_copy(src, j).start()

    def g_spread(src):
        for j in range(1, PLANE):
            g_copy(src, j).start()

    def h_line():
        return copy(hout, hin, line_send.at[0], line_recv.at[0], (pos + 1, me))

    def g_line():
        return copy(gout, gin, line_send.at[1], line_recv.at[1], (pos - 1, me))

    def find_back():
        total = None
        values = [gin[t].astype(jnp.float32) for t in range(tiles)]
        for k, off in enumerate(OFFS):
            flip = (-off[0], -off[1])
            moved = [shifted(v, flip, masks).astype(jnp.bfloat16) for v in values]
            term = dot(w_ref[k], jnp.concatenate(moved, axis=1), ((0,), (0,)))
            total = term if total is None else total + term
        for t in range(tiles):
            back[t] = total[:, t * pixels : (t + 1) * pixels]

    loads[0].wait()
    loads[1].wait()

    @pl.when(first)
    def _():
        h_spread(x_ref)
        hin[...] = x_ref[...]

    @pl.when(last)
    def _():
        g_spread(y_ref)
        gin[...] = y_ref[...]

    loads[2].wait()
    if sections > 1:

        @pl.when(last)
        def _():
            find_back()

        @pl.when(jnp.logical_not(first))
        def _():
            copy(hout, hin, line_send.at[0], line_recv.at[0], (pos - 1, me)).wait_recv()
            h_spread(hin)

        @pl.when(jnp.logical_not(last))
        def _():
            values = [act_of(hin[t]).astype(jnp.float32) for t in range(tiles)]
            total = None
            for k, off in enumerate(OFFS):
                moved = [shifted(v, off, masks).astype(jnp.bfloat16) for v in values]
                term = dot(w_ref[k], jnp.concatenate(moved, axis=1), ((1,), (0,)))
                total = term if total is None else total + term
            for t in range(tiles):
                piece = total[:, t * pixels : (t + 1) * pixels]
                hout[t] = (hin[t].astype(jnp.float32) + piece).astype(jnp.bfloat16)
            h_line().start()
            copy(gout, gin, line_send.at[1], line_recv.at[1], (pos + 1, me)).wait_recv()
            g_spread(gin)

        if sections > 2:

            @pl.when(jnp.logical_not(first) & jnp.logical_not(last))
            def _():
                find_back()

        @pl.when(jnp.logical_not(first))
        def _():
            for t in range(tiles):
                value = hin[t].astype(jnp.float32)
                sig = jax.nn.sigmoid(value)
                slope = sig * (1.0 + value * (1.0 - sig))
                gout[t] = (gin[t].astype(jnp.float32) + slope * back[t]).astype(jnp.bfloat16)
            g_line().start()

    def gradient(h_of, g_of):
        acts = jnp.concatenate([act_of(h_of(t)) for t in range(tiles)], axis=1)
        values = [g_of(t).astype(jnp.float32) for t in range(tiles)]
        stacked = []
        for off in OFFS:
            flip = (-off[0], -off[1])
            moved = [shifted(v, flip, masks).astype(jnp.bfloat16) for v in values]
            stacked.append(jnp.concatenate(moved, axis=1))
        return dot(jnp.concatenate(stacked, axis=0), acts, ((1,), (1,)))

    full = TAPS * rows
    wide = channels // LANES
    rest = channels - wide * LANES
    fits = LANES // rest
    tail = wide * full
    steady = TAPS // fits

    def place(k):
        if k < steady * fits:
            return tail + (k % steady) * rows, (k // steady) * rest
        return tail + (steady + k - steady * fits) * rows, 0

    def add_in(value, fresh):
        def put(start, piece):
            size = piece.shape[0]
            if fresh:
                acc[start : start + size, :] = piece
            else:
                acc[start : start + size, :] += piece

        for c in range(wide):
            put(c * full, value[:, c * LANES : (c + 1) * LANES])
        edge = value[:, wide * LANES :]
        span_rows = steady * rows
        sides = [edge[n * span_rows : (n + 1) * span_rows] for n in range(fits)]
        put(tail, jnp.concatenate(sides, axis=1))
        left = edge[fits * span_rows :]
        if left.shape[0]:
            put(tail + span_rows, jnp.concatenate([left] * fits, axis=1))

    mine = pl.multiple_of(quarter * rows, 16)
    add_in(gradient(lambda t: hin[t], lambda t: gin[t, pl.ds(mine, rows), :]), True)
    used = tail + (steady + TAPS - steady * fits) * rows
    if groups * chunk > used:
        acc[used:, :] = jnp.zeros((groups * chunk - used, LANES), jnp.float32)
    for j in range(1, PLANE):
        other, device = mate(j)
        copy(held_h.at[other], held_h.at[other], h_send.at[j], h_recv.at[other], device).wait_recv()
        copy(held_g.at[other], held_g.at[other], g_send.at[j], g_recv.at[other], device).wait_recv()
        add_in(gradient(lambda t: held_h[other, t], lambda t: held_g[other, t]), False)

    send_part[...] = acc[...].astype(jnp.bfloat16)

    def span(index):
        return pl.ds(pl.multiple_of(index * chunk, 16), chunk)

    def part_copy(i):
        other, device = column(i)
        return copy(send_part.at[span(other), :], got_part.at[group], part_send.at[i], part_recv.at[group], device)

    for i in range(1, groups):
        part_copy(i).start()
    total = acc[span(group), :]
    for i in range(1, groups):
        other, device = column(i)
        copy(got_part.at[other], got_part.at[other], part_send.at[i], part_recv.at[other], device).wait_recv()
        total = total + got_part[other].astype(jnp.float32)
    gathered[quarter, span(group), :] = total.astype(jnp.bfloat16)

    def block(source, part):
        return gathered.at[source, span(part), :]

    def z_copy(i):
        ref = block(quarter, group)
        return copy(ref, ref, z_send.at[i], all_recv.at[quarter, group], column(i)[1])

    def plane_copy(source, i, send_sem, j):
        part = column(i)[0]
        ref = block(source, part)
        return copy(ref, ref, send_sem, all_recv.at[source, part], mate(j)[1])

    def near(i, j):
        return plane_copy(quarter, i, near_send.at[j - 1, i], j)

    def far(i):
        if i % 2 == 0:
            return plane_copy(mate(1)[0], i, far_send.at[i], 2)
        return plane_copy(mate(2)[0], i, far_send.at[i], 1)

    def arrive(source, i):
        part = column(i)[0]
        ref = block(source, part)
        copy(ref, ref, far_send.at[i], all_recv.at[source, part], mate(1)[1]).wait_recv()

    for i in range(1, groups):
        z_copy(i).start()

    def relay(i):
        arrive(mate(1 if i % 2 == 0 else 2)[0], i)
        far(i).start()

    for i in range(groups):
        if i > 0:
            arrive(quarter, i)
        near(i, 1).start()
        near(i, 2).start()
        if i > 0:
            relay(i - 1)
    relay(groups - 1)
    def update(source):
        where = pl.ds(pl.multiple_of(source * rows, 16), rows)
        for k in range(TAPS):
            pieces = [(c * full + k * rows, 0, c * LANES, LANES) for c in range(wide)]
            pieces.append(place(k) + (wide * LANES, rest))
            for start, lane, column_at, width in pieces:
                grad = gathered[source, start : start + rows, lane : lane + width].astype(jnp.float32)
                cols = slice(column_at, column_at + width)
                new_m = momentum_rate * new_m_ref[k, where, cols] + grad
                new_m_ref[k, where, cols] = new_m
                old = w_ref[k, where, cols].astype(jnp.float32)
                new_w_ref[k, where, cols] = (old - learn_rate * new_m).astype(jnp.bfloat16)

    loads[3].wait()
    update(quarter)
    for j in (1, 2):
        for i in range(groups):
            if i % 2 == j - 1:
                continue
            arrive(mate(j)[0], i)
        update(mate(j)[0])
    for i in range(groups):
        arrive(mate(3)[0], i)
    update(mate(3)[0])
    for j in range(1, PLANE):
        h_copy(hin, j).wait_send()
        g_copy(gin, j).wait_send()
    for i in range(1, groups):
        part_copy(i).wait_send()
        z_copy(i).wait_send()
    for i in range(groups):
        near(i, 1).wait_send()
        near(i, 2).wait_send()
        far(i).wait_send()
    if sections > 1:

        @pl.when(jnp.logical_not(last))
        def _():
            h_line().wait_send()

        @pl.when(jnp.logical_not(first))
        def _():
            g_line().wait_send()


def shards(sections, count, inputs, out_grad, weights, momentum):
    channels, pixels = inputs.shape[2:]
    x = inputs.reshape((-1, channels, pixels))
    y = out_grad.reshape((-1, channels, pixels))
    tiles = x.shape[0]
    w = jnp.transpose(weights[0], (1, 0, 2))
    m = jnp.transpose(momentum[0], (1, 0, 2))
    groups = count // PLANE
    rows = channels // PLANE
    wide, rest = divmod(channels, LANES)
    fits = LANES // rest
    spare = TAPS // fits + TAPS % fits
    units = -(-((wide * TAPS + spare) * rows // 16) // groups)
    chunk = units * 16
    height = groups * chunk
    bf16, f32 = jnp.bfloat16, jnp.float32
    vmem = pl.BlockSpec(memory_space=pltpu.VMEM)
    dma = pltpu.SemaphoreType.DMA
    hbm = pl.BlockSpec(memory_space=pltpu.HBM)
    new_w, new_m = pl.pallas_call(
        functools.partial(step_kernel, sections, count, units),
        out_shape=(
            jax.ShapeDtypeStruct(w.shape, bf16),
            jax.ShapeDtypeStruct(w.shape, f32),
        ),
        in_specs=[hbm] * 4,
        out_specs=(vmem, vmem),
        scratch_shapes=[
            pltpu.VMEM((tiles, channels, pixels), bf16),
            pltpu.VMEM((tiles, channels, pixels), bf16),
            pltpu.VMEM(w.shape, bf16),
            pltpu.VMEM((tiles, channels, pixels), bf16),
            pltpu.VMEM((tiles, channels, pixels), bf16),
            pltpu.VMEM((tiles, channels, pixels), bf16),
            pltpu.VMEM((tiles, channels, pixels), bf16),
            pltpu.VMEM((tiles, channels, pixels), f32),
            pltpu.VMEM((PLANE, tiles, channels, pixels), bf16),
            pltpu.VMEM((PLANE, tiles, rows, pixels), bf16),
            pltpu.VMEM((height, LANES), f32),
            pltpu.VMEM((height, LANES), bf16),
            pltpu.VMEM((groups, chunk, LANES), bf16),
            pltpu.VMEM((PLANE, height, LANES), bf16),
            dma((2,)), dma((2,)), dma((PLANE,)), dma((PLANE,)), dma((PLANE,)), dma((PLANE,)),
            dma((groups,)), dma((groups,)), dma((groups,)), dma((PLANE, groups)),
            dma((2, groups)), dma((groups,)), dma((4,)),
        ],
        compiler_params=pltpu.CompilerParams(
            collective_id=0, has_side_effects=True, vmem_limit_bytes=40 * 1024 * 1024
        ),
    )(x, y, w, m)
    return jnp.transpose(new_w, (1, 0, 2))[None], jnp.transpose(new_m, (1, 0, 2))[None]


def solution(mesh):
    in_specs = (
        P(None, "dp", None, None),
        P(None, "dp", None, None),
        P("section", None, None, None),
        P("section", None, None, None),
    )
    out_specs = (P("section", None, None, None), P("section", None, None, None))
    body = functools.partial(shards, mesh.shape["section"], mesh.shape["dp"])
    return jax.shard_map(body, mesh=mesh, in_specs=in_specs, out_specs=out_specs, check_vma=False)
```

```python
import functools

import jax
import jax.numpy as jnp
from jax import lax
from jax.experimental import pallas as pl
from jax.experimental.pallas import tpu as pltpu
from jax.sharding import PartitionSpec as P

TILE_H = 8
TILE_W = 16
momentum_rate = 0.9
learn_rate = 0.02
MESH = pl.DeviceIdType.MESH
OFFS = [(i, j) for i in (-1, 0, 1) for j in (-1, 0, 1)]
TAPS = 9
PLANE = 4
LANES = 128


def masks_of(pixels):
    lane = lax.broadcasted_iota(jnp.int32, (1, pixels), 1)
    out = {}
    for off in OFFS:
        row = lane // TILE_W + off[0]
        col = lane % TILE_W + off[1]
        good = (row >= 0) & (row < TILE_H) & (col >= 0) & (col < TILE_W)
        out[off] = jnp.where(good, 1.0, 0.0)
    return out


def shifted(value, off, masks):
    if off == (0, 0):
        return value
    steps = -(off[0] * TILE_W + off[1]) % value.shape[-1]
    return pltpu.roll(value, steps, axis=1) * masks[off]


def dot(a, b, dims):
    return lax.dot_general(a, b, (dims, ((), ())), preferred_element_type=jnp.float32)


def act_of(hidden):
    value = hidden.astype(jnp.float32)
    return (value * jax.nn.sigmoid(value)).astype(jnp.bfloat16)


def step_kernel(
    sections, count, units,
    x_hbm, y_hbm, w_hbm, m_hbm, new_w_ref, new_m_ref,
    x_ref, y_ref, w_ref, hin, gin, hout, gout, back, held_h, held_g, acc, send_part, got_part, gathered,
    line_send, line_recv, h_send, h_recv, g_send, g_recv,
    part_send, part_recv, z_send, all_recv, near_send, far_send, diag_recv, load_sem,
):
    groups = count // PLANE
    pos = lax.axis_index("section")
    me = lax.axis_index("dp")
    quarter = lax.rem(me, PLANE)
    group = lax.div(me, PLANE)
    first = pos == 0
    last = pos == sections - 1
    tiles, channels, pixels = x_ref.shape
    loads = [
        pltpu.make_async_copy(src, dst, load_sem.at[n])
        for n, (src, dst) in enumerate(
            [(x_hbm, x_ref), (y_hbm, y_ref), (w_hbm, w_ref), (m_hbm, new_m_ref)]
        )
    ]
    for load in loads:
        load.start()
    rows = channels // PLANE
    chunk = units * 16
    masks = masks_of(pixels)

    def mate(j):
        other = jnp.bitwise_xor(quarter, j)
        return other, (pos, group * PLANE + other)

    def column(i):
        other = lax.rem(group + i, groups)
        return other, (pos, other * PLANE + quarter)

    barrier = pltpu.get_barrier_semaphore()

    def greet(device):
        pl.semaphore_signal(barrier, inc=1, device_id=device, device_id_type=MESH)

    for j in range(1, PLANE):
        greet(mate(j)[1])
    for i in range(1, groups):
        greet(column(i)[1])

    @pl.when(jnp.logical_not(first))
    def _():
        greet((pos - 1, me))

    @pl.when(jnp.logical_not(last))
    def _():
        greet((pos + 1, me))

    ends = jnp.where(first, 0, 1) + jnp.where(last, 0, 1)
    pl.semaphore_wait(barrier, PLANE - 1 + groups - 1 + ends)

    def copy(src, dst, send_sem, recv_sem, device):
        return pltpu.make_async_remote_copy(
            src_ref=src, dst_ref=dst, send_sem=send_sem, recv_sem=recv_sem,
            device_id=device, device_id_type=MESH,
        )

    def h_copy(src, j):
        return copy(src, held_h.at[quarter], h_send.at[j], h_recv.at[quarter], mate(j)[1])

    def g_copy(src, j):
        other, device = mate(j)
        start = pl.multiple_of(other * rows, 16)
        return copy(
            src.at[:, pl.ds(start, rows), :], held_g.at[quarter], g_send.at[j], g_recv.at[quarter], device
        )

    def h_spread(src):
        for j in range(1, PLANE):
            h_copy(src, j).start()

    def g_spread(src):
        for j in range(1, PLANE):
            g_copy(src, j).start()

    def h_line():
        return copy(hout, hin, line_send.at[0], line_recv.at[0], (pos + 1, me))

    def g_line():
        return copy(gout, gin, line_send.at[1], line_recv.at[1], (pos - 1, me))

    def find_back():
        total = None
        values = [gin[t].astype(jnp.float32) for t in range(tiles)]
        for k, off in enumerate(OFFS):
            flip = (-off[0], -off[1])
            moved = [shifted(v, flip, masks).astype(jnp.bfloat16) for v in values]
            term = dot(w_ref[k], jnp.concatenate(moved, axis=1), ((0,), (0,)))
            total = term if total is None else total + term
        for t in range(tiles):
            back[t] = total[:, t * pixels : (t + 1) * pixels]

    loads[0].wait()
    loads[1].wait()

    @pl.when(first)
    def _():
        h_spread(x_ref)
        hin[...] = x_ref[...]

    @pl.when(last)
    def _():
        g_spread(y_ref)
        gin[...] = y_ref[...]

    loads[2].wait()
    if sections > 1:

        @pl.when(last)
        def _():
            find_back()

        @pl.when(jnp.logical_not(first))
        def _():
            copy(hout, hin, line_send.at[0], line_recv.at[0], (pos - 1, me)).wait_recv()
            h_spread(hin)

        @pl.when(jnp.logical_not(last))
        def _():
            values = [act_of(hin[t]).astype(jnp.float32) for t in range(tiles)]
            total = None
            for k, off in enumerate(OFFS):
                moved = [shifted(v, off, masks).astype(jnp.bfloat16) for v in values]
                term = dot(w_ref[k], jnp.concatenate(moved, axis=1), ((1,), (0,)))
                total = term if total is None else total + term
            for t in range(tiles):
                piece = total[:, t * pixels : (t + 1) * pixels]
                hout[t] = (hin[t].astype(jnp.float32) + piece).astype(jnp.bfloat16)
            h_line().start()
            copy(gout, gin, line_send.at[1], line_recv.at[1], (pos + 1, me)).wait_recv()
            g_spread(gin)

        if sections > 2:

            @pl.when(jnp.logical_not(first) & jnp.logical_not(last))
            def _():
                find_back()

        @pl.when(jnp.logical_not(first))
        def _():
            for t in range(tiles):
                value = hin[t].astype(jnp.float32)
                sig = jax.nn.sigmoid(value)
                slope = sig * (1.0 + value * (1.0 - sig))
                gout[t] = (gin[t].astype(jnp.float32) + slope * back[t]).astype(jnp.bfloat16)
            g_line().start()

    def gradient(h_of, g_of):
        acts = jnp.concatenate([act_of(h_of(t)) for t in range(tiles)], axis=1)
        values = [g_of(t).astype(jnp.float32) for t in range(tiles)]
        stacked = []
        for off in OFFS:
            flip = (-off[0], -off[1])
            moved = [shifted(v, flip, masks).astype(jnp.bfloat16) for v in values]
            stacked.append(jnp.concatenate(moved, axis=1))
        return dot(jnp.concatenate(stacked, axis=0), acts, ((1,), (1,)))

    full = TAPS * rows
    wide = channels // LANES
    rest = channels - wide * LANES
    fits = LANES // rest
    tail = wide * full
    steady = TAPS // fits

    def place(k):
        if k < steady * fits:
            return tail + (k % steady) * rows, (k // steady) * rest
        return tail + (steady + k - steady * fits) * rows, 0

    def add_in(value, fresh):
        def put(start, piece):
            size = piece.shape[0]
            if fresh:
                acc[start : start + size, :] = piece
            else:
                acc[start : start + size, :] += piece

        for c in range(wide):
            put(c * full, value[:, c * LANES : (c + 1) * LANES])
        edge = value[:, wide * LANES :]
        span_rows = steady * rows
        sides = [edge[n * span_rows : (n + 1) * span_rows] for n in range(fits)]
        put(tail, jnp.concatenate(sides, axis=1))
        left = edge[fits * span_rows :]
        if left.shape[0]:
            put(tail + span_rows, jnp.concatenate([left] * fits, axis=1))

    mine = pl.multiple_of(quarter * rows, 16)
    add_in(gradient(lambda t: hin[t], lambda t: gin[t, pl.ds(mine, rows), :]), True)
    used = tail + (steady + TAPS - steady * fits) * rows
    if groups * chunk > used:
        acc[used:, :] = jnp.zeros((groups * chunk - used, LANES), jnp.float32)
    for j in range(1, PLANE):
        other, device = mate(j)
        copy(held_h.at[other], held_h.at[other], h_send.at[j], h_recv.at[other], device).wait_recv()
        copy(held_g.at[other], held_g.at[other], g_send.at[j], g_recv.at[other], device).wait_recv()
        add_in(gradient(lambda t: held_h[other, t], lambda t: held_g[other, t]), False)

    send_part[...] = acc[...].astype(jnp.bfloat16)

    def span(index):
        return pl.ds(pl.multiple_of(index * chunk, 16), chunk)

    def part_copy(i):
        other, device = column(i)
        return copy(send_part.at[span(other), :], got_part.at[group], part_send.at[i], part_recv.at[group], device)

    for i in range(1, groups):
        part_copy(i).start()
    total = acc[span(group), :]
    for i in range(1, groups):
        other, device = column(i)
        copy(got_part.at[other], got_part.at[other], part_send.at[i], part_recv.at[other], device).wait_recv()
        total = total + got_part[other].astype(jnp.float32)
    gathered[quarter, span(group), :] = total.astype(jnp.bfloat16)

    def block(source, part):
        return gathered.at[source, span(part), :]

    halves = [(0, (units + 1) // 2 * 16), ((units + 1) // 2 * 16, units // 2 * 16)]
    sides = [-1, 1]

    def side_part(s, side):
        part = group + sides[side] * s
        return part, (part >= 0) & (part < groups)

    def side_open(side):
        other = group - sides[side]
        return (other >= 0) & (other < groups)

    def chain_copy(s, side):
        part = side_part(s, side)[0]
        ref = block(quarter, part)
        device = (pos, (group - sides[side]) * PLANE + quarter)
        return copy(ref, ref, z_send.at[side, s], all_recv.at[quarter, part], device)

    def near(part, j):
        ref = block(quarter, part)
        return copy(ref, ref, near_send.at[j - 1, part], all_recv.at[quarter, part], mate(j)[1])

    def half_block(source, part, half):
        start, size = halves[half]
        return gathered.at[source, pl.ds(pl.multiple_of(part * chunk + start, 16), size), :]

    def far(part, half):
        ref = half_block(mate(half + 1)[0], part, half)
        return copy(ref, ref, far_send.at[half, part], diag_recv.at[half, part], mate(2 - half)[1])

    def arrive(source, part):
        ref = block(source, part)
        copy(ref, ref, z_send.at[0, 0], all_recv.at[source, part], mate(1)[1]).wait_recv()

    def arrive_diag(part, half):
        ref = half_block(mate(3)[0], part, half)
        copy(ref, ref, far_send.at[half, part], diag_recv.at[half, part], mate(1)[1]).wait_recv()

    def near_both(part):
        near(part, 1).start()
        near(part, 2).start()

    def relay(part):
        for half in range(2):
            arrive(mate(half + 1)[0], part)
            far(part, half).start()

    for s in range(groups):
        for side in range(2):
            part, valid = side_part(s, side)
            if s:

                @pl.when(valid)
                def _():
                    arrive(quarter, part)

            @pl.when(valid & side_open(side))
            def _():
                chain_copy(s, side).start()

            if s == 0:
                if side == 1:
                    near_both(group)
                continue

            @pl.when(valid)
            def _():
                near_both(part)

        if s == 1:
            relay(group)
        elif s > 1:
            for side in range(2):
                part, valid = side_part(s - 1, side)

                @pl.when(valid)
                def _():
                    relay(part)

    if groups == 1:
        relay(group)
    else:
        for side in range(2):
            part, valid = side_part(groups - 1, side)

            @pl.when(valid)
            def _():
                relay(part)

    def update(source):
        where = pl.ds(pl.multiple_of(source * rows, 16), rows)
        for k in range(TAPS):
            pieces = [(c * full + k * rows, 0, c * LANES, LANES) for c in range(wide)]
            pieces.append(place(k) + (wide * LANES, rest))
            for start, lane, column_at, width in pieces:
                grad = gathered[source, start : start + rows, lane : lane + width].astype(jnp.float32)
                cols = slice(column_at, column_at + width)
                new_m = momentum_rate * new_m_ref[k, where, cols] + grad
                new_m_ref[k, where, cols] = new_m
                old = w_ref[k, where, cols].astype(jnp.float32)
                new_w_ref[k, where, cols] = (old - learn_rate * new_m).astype(jnp.bfloat16)

    loads[3].wait()
    update(quarter)
    update(mate(1)[0])
    update(mate(2)[0])
    for part in range(groups):
        arrive_diag(part, 0)
        arrive_diag(part, 1)
    update(mate(3)[0])
    for j in range(1, PLANE):
        h_copy(hin, j).wait_send()
        g_copy(gin, j).wait_send()
    for i in range(1, groups):
        part_copy(i).wait_send()
    for part in range(groups):
        for n in range(2):
            near(part, n + 1).wait_send()
            far(part, n).wait_send()
    for s in range(groups):
        for side in range(2):

            @pl.when(side_part(s, side)[1] & side_open(side))
            def _():
                chain_copy(s, side).wait_send()

    if sections > 1:

        @pl.when(jnp.logical_not(last))
        def _():
            h_line().wait_send()

        @pl.when(jnp.logical_not(first))
        def _():
            g_line().wait_send()


def shards(sections, count, inputs, out_grad, weights, momentum):
    channels, pixels = inputs.shape[2:]
    x = inputs.reshape((-1, channels, pixels))
    y = out_grad.reshape((-1, channels, pixels))
    tiles = x.shape[0]
    w = jnp.transpose(weights[0], (1, 0, 2))
    m = jnp.transpose(momentum[0], (1, 0, 2))
    groups = count // PLANE
    rows = channels // PLANE
    wide, rest = divmod(channels, LANES)
    fits = LANES // rest
    spare = TAPS // fits + TAPS % fits
    units = -(-((wide * TAPS + spare) * rows // 16) // groups)
    chunk = units * 16
    height = groups * chunk
    bf16, f32 = jnp.bfloat16, jnp.float32
    vmem = pl.BlockSpec(memory_space=pltpu.VMEM)
    dma = pltpu.SemaphoreType.DMA
    hbm = pl.BlockSpec(memory_space=pltpu.HBM)
    new_w, new_m = pl.pallas_call(
        functools.partial(step_kernel, sections, count, units),
        out_shape=(
            jax.ShapeDtypeStruct(w.shape, bf16),
            jax.ShapeDtypeStruct(w.shape, f32),
        ),
        in_specs=[hbm] * 4,
        out_specs=(vmem, vmem),
        scratch_shapes=[
            pltpu.VMEM((tiles, channels, pixels), bf16),
            pltpu.VMEM((tiles, channels, pixels), bf16),
            pltpu.VMEM(w.shape, bf16),
            pltpu.VMEM((tiles, channels, pixels), bf16),
            pltpu.VMEM((tiles, channels, pixels), bf16),
            pltpu.VMEM((tiles, channels, pixels), bf16),
            pltpu.VMEM((tiles, channels, pixels), bf16),
            pltpu.VMEM((tiles, channels, pixels), f32),
            pltpu.VMEM((PLANE, tiles, channels, pixels), bf16),
            pltpu.VMEM((PLANE, tiles, rows, pixels), bf16),
            pltpu.VMEM((height, LANES), f32),
            pltpu.VMEM((height, LANES), bf16),
            pltpu.VMEM((groups, chunk, LANES), bf16),
            pltpu.VMEM((PLANE, height, LANES), bf16),
            dma((2,)), dma((2,)), dma((PLANE,)), dma((PLANE,)), dma((PLANE,)), dma((PLANE,)),
            dma((groups,)), dma((groups,)), dma((2, groups)), dma((PLANE, groups)),
            dma((2, groups)), dma((2, groups)), dma((2, groups)), dma((4,)),
        ],
        compiler_params=pltpu.CompilerParams(
            collective_id=0, has_side_effects=True, vmem_limit_bytes=44 * 1024 * 1024
        ),
    )(*[pltpu.with_memory_space_constraint(v, pltpu.HBM) for v in (x, y, w, m)])
    return jnp.transpose(new_w, (1, 0, 2))[None], jnp.transpose(new_m, (1, 0, 2))[None]


def solution(mesh):
    in_specs = (
        P(None, "dp", None, None),
        P(None, "dp", None, None),
        P("section", None, None, None),
        P("section", None, None, None),
    )
    out_specs = (P("section", None, None, None), P("section", None, None, None))
    body = functools.partial(shards, mesh.shape["section"], mesh.shape["dp"])
    return jax.shard_map(body, mesh=mesh, in_specs=in_specs, out_specs=out_specs, check_vma=False)
```

```python
import functools

import jax
import jax.numpy as jnp
from jax import lax
from jax.experimental import pallas as pl
from jax.experimental.pallas import tpu as pltpu
from jax.sharding import PartitionSpec as P

TILE_H = 8
TILE_W = 16
momentum_rate = 0.9
learn_rate = 0.02
MESH = pl.DeviceIdType.MESH
OFFS = [(i, j) for i in (-1, 0, 1) for j in (-1, 0, 1)]
TAPS = 9
PLANE = 4
LANES = 128


def masks_of(pixels):
    lane = lax.broadcasted_iota(jnp.int32, (1, pixels), 1)
    out = {}
    for off in OFFS:
        row = lane // TILE_W + off[0]
        col = lane % TILE_W + off[1]
        good = (row >= 0) & (row < TILE_H) & (col >= 0) & (col < TILE_W)
        out[off] = jnp.where(good, 1.0, 0.0)
    return out


def shifted(value, off, masks):
    if off == (0, 0):
        return value
    steps = -(off[0] * TILE_W + off[1]) % value.shape[-1]
    return pltpu.roll(value, steps, axis=1) * masks[off]


def dot(a, b, dims):
    return lax.dot_general(a, b, (dims, ((), ())), preferred_element_type=jnp.float32)


def act_of(hidden):
    value = hidden.astype(jnp.float32)
    return (value * jax.nn.sigmoid(value)).astype(jnp.bfloat16)


def step_kernel(
    sections, count, units,
    x_hbm, y_hbm, w_hbm, m_hbm, new_w_ref, new_m_ref,
    x_ref, y_ref, w_ref, hin, gin, hout, gout, back, held_h, held_g, cols, acts, stacks, acc, send_part, got_part, gathered,
    line_send, line_recv, h_send, h_recv, g_send, g_recv,
    part_send, part_recv, z_send, all_recv, near_send, far_send, diag_recv, load_sem,
):
    groups = count // PLANE
    pos = lax.axis_index("section")
    me = lax.axis_index("dp")
    quarter = lax.rem(me, PLANE)
    group = lax.div(me, PLANE)
    first = pos == 0
    last = pos == sections - 1
    tiles, channels, pixels = x_ref.shape
    loads = [
        pltpu.make_async_copy(src, dst, load_sem.at[n])
        for n, (src, dst) in enumerate(
            [(x_hbm, x_ref), (y_hbm, y_ref), (w_hbm, w_ref), (m_hbm, new_m_ref)]
        )
    ]
    for load in loads:
        load.start()
    rows = channels // PLANE
    chunk = units * 16
    masks = masks_of(pixels)

    def mate(j):
        other = jnp.bitwise_xor(quarter, j)
        return other, (pos, group * PLANE + other)

    def column(i):
        other = lax.rem(group + i, groups)
        return other, (pos, other * PLANE + quarter)

    barrier = pltpu.get_barrier_semaphore()

    def greet(device):
        pl.semaphore_signal(barrier, inc=1, device_id=device, device_id_type=MESH)

    for j in range(1, PLANE):
        greet(mate(j)[1])
    for i in range(1, groups):
        greet(column(i)[1])

    @pl.when(jnp.logical_not(first))
    def _():
        greet((pos - 1, me))

    @pl.when(jnp.logical_not(last))
    def _():
        greet((pos + 1, me))

    ends = jnp.where(first, 0, 1) + jnp.where(last, 0, 1)

    def spread_taps(values, turn):
        for k, off in enumerate(OFFS):
            flip = (turn * off[0], turn * off[1])
            moved = [shifted(v, flip, masks).astype(jnp.bfloat16) for v in values]
            cols[k] = jnp.concatenate(moved, axis=1)

    def h_taps():
        spread_taps([act_of(hin[t]).astype(jnp.float32) for t in range(tiles)], 1)

    def g_taps():
        spread_taps([gin[t].astype(jnp.float32) for t in range(tiles)], -1)

    loads[0].wait()
    loads[1].wait()

    @pl.when(first)
    def _():
        hin[...] = x_ref[...]
        if sections > 1:
            h_taps()

    @pl.when(last)
    def _():
        gin[...] = y_ref[...]
        if sections > 1:
            g_taps()

    pl.semaphore_wait(barrier, PLANE - 1 + groups - 1 + ends)

    def copy(src, dst, send_sem, recv_sem, device):
        return pltpu.make_async_remote_copy(
            src_ref=src, dst_ref=dst, send_sem=send_sem, recv_sem=recv_sem,
            device_id=device, device_id_type=MESH,
        )

    def h_copy(src, j):
        return copy(src, held_h.at[quarter], h_send.at[j], h_recv.at[quarter], mate(j)[1])

    def g_copy(src, j):
        other, device = mate(j)
        start = pl.multiple_of(other * rows, 16)
        return copy(
            src.at[:, pl.ds(start, rows), :], held_g.at[quarter], g_send.at[j], g_recv.at[quarter], device
        )

    def h_spread(src):
        for j in range(1, PLANE):
            h_copy(src, j).start()

    def g_spread(src):
        for j in range(1, PLANE):
            g_copy(src, j).start()

    def h_line():
        return copy(hout, hin, line_send.at[0], line_recv.at[0], (pos + 1, me))

    def g_line():
        return copy(gout, gin, line_send.at[1], line_recv.at[1], (pos - 1, me))

    mine = pl.multiple_of(quarter * rows, 16)

    def take_act(j):
        if j:
            other, device = mate(j)
            copy(held_h.at[other], held_h.at[other], h_send.at[j], h_recv.at[other], device).wait_recv()
        hs = [held_h[other, t] if j else hin[t] for t in range(tiles)]
        acts[j] = jnp.concatenate([act_of(h) for h in hs], axis=1)

    def take_stack(j):
        if j:
            other, device = mate(j)
            copy(held_g.at[other], held_g.at[other], g_send.at[j], g_recv.at[other], device).wait_recv()
        gs = [held_g[other, t] if j else gin[t, pl.ds(mine, rows), :] for t in range(tiles)]
        values = [g.astype(jnp.float32) for g in gs]
        for k, off in enumerate(OFFS):
            flip = (-off[0], -off[1])
            moved = [shifted(v, flip, masks).astype(jnp.bfloat16) for v in values]
            stacks[j, k * rows : (k + 1) * rows, :] = jnp.concatenate(moved, axis=1)

    def find_back():
        total = None
        for k in range(TAPS):
            term = dot(w_ref[k], cols[k], ((0,), (0,)))
            total = term if total is None else total + term
        for t in range(tiles):
            back[t] = total[:, t * pixels : (t + 1) * pixels]

    @pl.when(first)
    def _():
        h_spread(x_ref)

    @pl.when(last)
    def _():
        g_spread(y_ref)

    loads[2].wait()
    if sections > 1:

        @pl.when(last)
        def _():
            find_back()

        @pl.when(jnp.logical_not(first))
        def _():
            copy(hout, hin, line_send.at[0], line_recv.at[0], (pos - 1, me)).wait_recv()
            h_spread(hin)

        @pl.when(jnp.logical_not(last))
        def _():
            if sections > 2:

                @pl.when(jnp.logical_not(first))
                def _():
                    h_taps()

            total = None
            for k in range(TAPS):
                term = dot(w_ref[k], cols[k], ((1,), (0,)))
                total = term if total is None else total + term
            for t in range(tiles):
                piece = total[:, t * pixels : (t + 1) * pixels]
                hout[t] = (hin[t].astype(jnp.float32) + piece).astype(jnp.bfloat16)
            h_line().start()

        @pl.when(first)
        def _():
            for j in range(PLANE):
                take_act(j)

        @pl.when(jnp.logical_not(last))
        def _():
            copy(gout, gin, line_send.at[1], line_recv.at[1], (pos + 1, me)).wait_recv()
            g_spread(gin)

        if sections > 2:

            @pl.when(jnp.logical_not(first) & jnp.logical_not(last))
            def _():
                g_taps()
                find_back()

        @pl.when(jnp.logical_not(first))
        def _():
            for t in range(tiles):
                value = hin[t].astype(jnp.float32)
                sig = jax.nn.sigmoid(value)
                slope = sig * (1.0 + value * (1.0 - sig))
                gout[t] = (gin[t].astype(jnp.float32) + slope * back[t]).astype(jnp.bfloat16)
            g_line().start()

    def gradient(j):
        return dot(stacks[j], acts[j], ((1,), (1,)))

    full = TAPS * rows
    wide = channels // LANES
    rest = channels - wide * LANES
    fits = LANES // rest
    tail = wide * full
    steady = TAPS // fits

    def place(k):
        if k < steady * fits:
            return tail + (k % steady) * rows, (k // steady) * rest
        return tail + (steady + k - steady * fits) * rows, 0

    def add_in(value, fresh):
        def put(start, piece):
            size = piece.shape[0]
            if fresh:
                acc[start : start + size, :] = piece
            else:
                acc[start : start + size, :] += piece

        for c in range(wide):
            put(c * full, value[:, c * LANES : (c + 1) * LANES])
        edge = value[:, wide * LANES :]
        span_rows = steady * rows
        sides = [edge[n * span_rows : (n + 1) * span_rows] for n in range(fits)]
        put(tail, jnp.concatenate(sides, axis=1))
        left = edge[fits * span_rows :]
        if left.shape[0]:
            put(tail + span_rows, jnp.concatenate([left] * fits, axis=1))

    used = tail + (steady + TAPS - steady * fits) * rows
    if groups * chunk > used:
        acc[used:, :] = jnp.zeros((groups * chunk - used, LANES), jnp.float32)
    @pl.when(last)
    def _():
        for j in range(PLANE):
            take_stack(j)

    for j in range(PLANE):
        if sections > 1:

            @pl.when(jnp.logical_not(first))
            def _():
                take_act(j)

        else:
            take_act(j)

        @pl.when(jnp.logical_not(last))
        def _():
            take_stack(j)

        add_in(gradient(j), j == 0)

    send_part[...] = acc[...].astype(jnp.bfloat16)

    def span(index):
        return pl.ds(pl.multiple_of(index * chunk, 16), chunk)

    def part_copy(i):
        other, device = column(i)
        return copy(send_part.at[span(other), :], got_part.at[group], part_send.at[i], part_recv.at[group], device)

    for i in range(1, groups):
        part_copy(i).start()
    total = acc[span(group), :]
    for i in range(1, groups):
        other, device = column(i)
        copy(got_part.at[other], got_part.at[other], part_send.at[i], part_recv.at[other], device).wait_recv()
        total = total + got_part[other].astype(jnp.float32)
    gathered[quarter, span(group), :] = total.astype(jnp.bfloat16)

    def block(source, part):
        return gathered.at[source, span(part), :]

    halves = [(0, (units + 1) // 2 * 16), ((units + 1) // 2 * 16, units // 2 * 16)]
    sides = [-1, 1]

    def side_part(s, side):
        part = group + sides[side] * s
        return part, (part >= 0) & (part < groups)

    def side_open(side):
        other = group - sides[side]
        return (other >= 0) & (other < groups)

    def chain_copy(s, side):
        part = side_part(s, side)[0]
        ref = block(quarter, part)
        device = (pos, (group - sides[side]) * PLANE + quarter)
        return copy(ref, ref, z_send.at[side, s], all_recv.at[quarter, part], device)

    def near(part, j):
        ref = block(quarter, part)
        return copy(ref, ref, near_send.at[j - 1, part], all_recv.at[quarter, part], mate(j)[1])

    def half_block(source, part, half):
        start, size = halves[half]
        return gathered.at[source, pl.ds(pl.multiple_of(part * chunk + start, 16), size), :]

    def far(part, half):
        ref = half_block(mate(half + 1)[0], part, half)
        return copy(ref, ref, far_send.at[half, part], diag_recv.at[half, part], mate(2 - half)[1])

    def arrive(source, part):
        ref = block(source, part)
        copy(ref, ref, z_send.at[0, 0], all_recv.at[source, part], mate(1)[1]).wait_recv()

    def arrive_diag(part, half):
        ref = half_block(mate(3)[0], part, half)
        copy(ref, ref, far_send.at[half, part], diag_recv.at[half, part], mate(1)[1]).wait_recv()

    def near_both(part):
        near(part, 1).start()
        near(part, 2).start()

    def relay(part):
        for half in range(2):
            arrive(mate(half + 1)[0], part)
            far(part, half).start()

    for s in range(groups):
        for side in range(2):
            part, valid = side_part(s, side)
            if s:

                @pl.when(valid)
                def _():
                    arrive(quarter, part)

            @pl.when(valid & side_open(side))
            def _():
                chain_copy(s, side).start()

            if s == 0:
                if side == 1:
                    near_both(group)
                continue

            @pl.when(valid)
            def _():
                near_both(part)

        if s == 1:
            relay(group)
        elif s > 1:
            for side in range(2):
                part, valid = side_part(s - 1, side)

                @pl.when(valid)
                def _():
                    relay(part)

    if groups == 1:
        relay(group)
    else:
        for side in range(2):
            part, valid = side_part(groups - 1, side)

            @pl.when(valid)
            def _():
                relay(part)

    def update(source):
        where = pl.ds(pl.multiple_of(source * rows, 16), rows)
        for k in range(TAPS):
            pieces = [(c * full + k * rows, 0, c * LANES, LANES) for c in range(wide)]
            pieces.append(place(k) + (wide * LANES, rest))
            for start, lane, column_at, width in pieces:
                grad = gathered[source, start : start + rows, lane : lane + width].astype(jnp.float32)
                cols = slice(column_at, column_at + width)
                new_m = momentum_rate * new_m_ref[k, where, cols] + grad
                new_m_ref[k, where, cols] = new_m
                old = w_ref[k, where, cols].astype(jnp.float32)
                new_w_ref[k, where, cols] = (old - learn_rate * new_m).astype(jnp.bfloat16)

    loads[3].wait()
    update(quarter)
    update(mate(1)[0])
    update(mate(2)[0])
    for part in range(groups):
        arrive_diag(part, 0)
        arrive_diag(part, 1)
    update(mate(3)[0])
    for j in range(1, PLANE):
        h_copy(hin, j).wait_send()
        g_copy(gin, j).wait_send()
    for i in range(1, groups):
        part_copy(i).wait_send()
    for part in range(groups):
        for n in range(2):
            near(part, n + 1).wait_send()
            far(part, n).wait_send()
    for s in range(groups):
        for side in range(2):

            @pl.when(side_part(s, side)[1] & side_open(side))
            def _():
                chain_copy(s, side).wait_send()

    if sections > 1:

        @pl.when(jnp.logical_not(last))
        def _():
            h_line().wait_send()

        @pl.when(jnp.logical_not(first))
        def _():
            g_line().wait_send()


def shards(sections, count, inputs, out_grad, weights, momentum):
    channels, pixels = inputs.shape[2:]
    x = inputs.reshape((-1, channels, pixels))
    y = out_grad.reshape((-1, channels, pixels))
    tiles = x.shape[0]
    w = jnp.transpose(weights[0], (1, 0, 2))
    m = jnp.transpose(momentum[0], (1, 0, 2))
    groups = count // PLANE
    rows = channels // PLANE
    wide, rest = divmod(channels, LANES)
    fits = LANES // rest
    spare = TAPS // fits + TAPS % fits
    units = -(-((wide * TAPS + spare) * rows // 16) // groups)
    chunk = units * 16
    height = groups * chunk
    bf16, f32 = jnp.bfloat16, jnp.float32
    vmem = pl.BlockSpec(memory_space=pltpu.VMEM)
    dma = pltpu.SemaphoreType.DMA
    hbm = pl.BlockSpec(memory_space=pltpu.HBM)
    new_w, new_m = pl.pallas_call(
        functools.partial(step_kernel, sections, count, units),
        out_shape=(
            jax.ShapeDtypeStruct(w.shape, bf16),
            jax.ShapeDtypeStruct(w.shape, f32),
        ),
        in_specs=[hbm] * 4,
        out_specs=(vmem, vmem),
        scratch_shapes=[
            pltpu.VMEM((tiles, channels, pixels), bf16),
            pltpu.VMEM((tiles, channels, pixels), bf16),
            pltpu.VMEM(w.shape, bf16),
            pltpu.VMEM((tiles, channels, pixels), bf16),
            pltpu.VMEM((tiles, channels, pixels), bf16),
            pltpu.VMEM((tiles, channels, pixels), bf16),
            pltpu.VMEM((tiles, channels, pixels), bf16),
            pltpu.VMEM((tiles, channels, pixels), f32),
            pltpu.VMEM((PLANE, tiles, channels, pixels), bf16),
            pltpu.VMEM((PLANE, tiles, rows, pixels), bf16),
            pltpu.VMEM((TAPS, channels, tiles * pixels), bf16),
            pltpu.VMEM((PLANE, channels, tiles * pixels), bf16),
            pltpu.VMEM((PLANE, TAPS * rows, tiles * pixels), bf16),
            pltpu.VMEM((height, LANES), f32),
            pltpu.VMEM((height, LANES), bf16),
            pltpu.VMEM((groups, chunk, LANES), bf16),
            pltpu.VMEM((PLANE, height, LANES), bf16),
            dma((2,)), dma((2,)), dma((PLANE,)), dma((PLANE,)), dma((PLANE,)), dma((PLANE,)),
            dma((groups,)), dma((groups,)), dma((2, groups)), dma((PLANE, groups)),
            dma((2, groups)), dma((2, groups)), dma((2, groups)), dma((4,)),
        ],
        compiler_params=pltpu.CompilerParams(
            collective_id=0, has_side_effects=True, vmem_limit_bytes=44 * 1024 * 1024
        ),
    )(*[pltpu.with_memory_space_constraint(v, pltpu.HBM) for v in (x, y, w, m)])
    return jnp.transpose(new_w, (1, 0, 2))[None], jnp.transpose(new_m, (1, 0, 2))[None]


def solution(mesh):
    in_specs = (
        P(None, "dp", None, None),
        P(None, "dp", None, None),
        P("section", None, None, None),
        P("section", None, None, None),
    )
    out_specs = (P("section", None, None, None), P("section", None, None, None))
    body = functools.partial(shards, mesh.shape["section"], mesh.shape["dp"])
    return jax.shard_map(body, mesh=mesh, in_specs=in_specs, out_specs=out_specs, check_vma=False)
```

```python
import functools

import jax
import jax.numpy as jnp
from jax import lax
from jax.experimental import pallas as pl
from jax.experimental.pallas import tpu as pltpu
from jax.sharding import PartitionSpec as P

TILE_H = 8
TILE_W = 16
momentum_rate = 0.9
learn_rate = 0.02
MESH = pl.DeviceIdType.MESH
OFFS = [(i, j) for i in (-1, 0, 1) for j in (-1, 0, 1)]
TAPS = 9
PLANE = 4
LANES = 128


def masks_of(pixels):
    lane = lax.broadcasted_iota(jnp.int32, (1, pixels), 1)
    out = {}
    for off in OFFS:
        row = lane // TILE_W + off[0]
        col = lane % TILE_W + off[1]
        good = (row >= 0) & (row < TILE_H) & (col >= 0) & (col < TILE_W)
        out[off] = jnp.where(good, 1.0, 0.0)
    return out


def shifted(value, off, masks):
    if off == (0, 0):
        return value
    steps = -(off[0] * TILE_W + off[1]) % value.shape[-1]
    return pltpu.roll(value, steps, axis=1) * masks[off]


def dot(a, b, dims):
    return lax.dot_general(a, b, (dims, ((), ())), preferred_element_type=jnp.float32)


def act_of(hidden):
    value = hidden.astype(jnp.float32)
    return (value * jax.nn.sigmoid(value)).astype(jnp.bfloat16)


def step_kernel(
    sections, count, units,
    x_hbm, y_hbm, w_hbm, m_hbm, new_w_ref, new_m_ref,
    x_ref, y_ref, w_ref, hin, gin, hout, gout, back, held_h, held_g, cols, acts, stacks, acc, send_part, got_part, gathered,
    line_send, line_recv, h_send, h_recv, g_send, g_recv,
    part_send, part_recv, z_send, all_recv, near_send, far_send, diag_recv, load_sem,
):
    groups = count // PLANE
    pos = lax.axis_index("section")
    me = lax.axis_index("dp")
    quarter = lax.rem(me, PLANE)
    group = lax.div(me, PLANE)
    first = pos == 0
    last = pos == sections - 1
    tiles, channels, pixels = x_ref.shape
    loads = [
        pltpu.make_async_copy(src, dst, load_sem.at[n])
        for n, (src, dst) in enumerate(
            [(x_hbm, x_ref), (y_hbm, y_ref), (w_hbm, w_ref), (m_hbm, new_m_ref)]
        )
    ]
    for load in loads:
        load.start()
    rows = channels // PLANE
    chunk = units * 16
    masks = masks_of(pixels)

    def mate(j):
        other = jnp.bitwise_xor(quarter, j)
        return other, (pos, group * PLANE + other)

    def column(i):
        other = lax.rem(group + i, groups)
        return other, (pos, other * PLANE + quarter)

    barrier = pltpu.get_barrier_semaphore()

    def greet(device):
        pl.semaphore_signal(barrier, inc=1, device_id=device, device_id_type=MESH)

    for j in range(1, PLANE):
        greet(mate(j)[1])
    for i in range(1, groups):
        greet(column(i)[1])

    @pl.when(jnp.logical_not(first))
    def _():
        greet((pos - 1, me))

    @pl.when(jnp.logical_not(last))
    def _():
        greet((pos + 1, me))

    ends = jnp.where(first, 0, 1) + jnp.where(last, 0, 1)

    def spread_taps(values, turn):
        for k, off in enumerate(OFFS):
            flip = (turn * off[0], turn * off[1])
            moved = [shifted(v, flip, masks).astype(jnp.bfloat16) for v in values]
            cols[k] = jnp.concatenate(moved, axis=1)

    def h_taps():
        spread_taps([act_of(hin[t]).astype(jnp.float32) for t in range(tiles)], 1)

    def g_taps():
        spread_taps([gin[t].astype(jnp.float32) for t in range(tiles)], -1)

    loads[0].wait()
    loads[1].wait()

    @pl.when(first)
    def _():
        hin[...] = x_ref[...]
        if sections > 1:
            h_taps()

    @pl.when(last)
    def _():
        gin[...] = y_ref[...]
        if sections > 1:
            g_taps()

    pl.semaphore_wait(barrier, PLANE - 1 + groups - 1 + ends)

    def copy(src, dst, send_sem, recv_sem, device):
        return pltpu.make_async_remote_copy(
            src_ref=src, dst_ref=dst, send_sem=send_sem, recv_sem=recv_sem,
            device_id=device, device_id_type=MESH,
        )

    def h_copy(src, j):
        return copy(src, held_h.at[quarter], h_send.at[j], h_recv.at[quarter], mate(j)[1])

    def g_copy(src, j):
        other, device = mate(j)
        start = pl.multiple_of(other * rows, 16)
        return copy(
            src.at[:, pl.ds(start, rows), :], held_g.at[quarter], g_send.at[j], g_recv.at[quarter], device
        )

    def h_spread(src):
        for j in range(1, PLANE):
            h_copy(src, j).start()

    def g_spread(src):
        for j in range(1, PLANE):
            g_copy(src, j).start()

    def h_line():
        return copy(hout, hin, line_send.at[0], line_recv.at[0], (pos + 1, me))

    def g_line():
        return copy(gout, gin, line_send.at[1], line_recv.at[1], (pos - 1, me))

    mine = pl.multiple_of(quarter * rows, 16)

    def take_act(j):
        if j:
            other, device = mate(j)
            copy(held_h.at[other], held_h.at[other], h_send.at[j], h_recv.at[other], device).wait_recv()
        hs = [held_h[other, t] if j else hin[t] for t in range(tiles)]
        acts[j] = jnp.concatenate([act_of(h) for h in hs], axis=1)

    def take_stack(j):
        if j:
            other, device = mate(j)
            copy(held_g.at[other], held_g.at[other], g_send.at[j], g_recv.at[other], device).wait_recv()
        gs = [held_g[other, t] if j else gin[t, pl.ds(mine, rows), :] for t in range(tiles)]
        values = [g.astype(jnp.float32) for g in gs]
        for k, off in enumerate(OFFS):
            flip = (-off[0], -off[1])
            moved = [shifted(v, flip, masks).astype(jnp.bfloat16) for v in values]
            stacks[j, k * rows : (k + 1) * rows, :] = jnp.concatenate(moved, axis=1)

    def find_back():
        total = None
        for k in range(TAPS):
            term = dot(w_ref[k], cols[k], ((0,), (0,)))
            total = term if total is None else total + term
        for t in range(tiles):
            back[t] = total[:, t * pixels : (t + 1) * pixels]

    @pl.when(first)
    def _():
        h_spread(x_ref)

    @pl.when(last)
    def _():
        g_spread(y_ref)

    loads[2].wait()
    if sections > 1:

        @pl.when(last)
        def _():
            find_back()

        @pl.when(jnp.logical_not(first))
        def _():
            copy(hout, hin, line_send.at[0], line_recv.at[0], (pos - 1, me)).wait_recv()
            h_spread(hin)

        @pl.when(jnp.logical_not(last))
        def _():
            if sections > 2:

                @pl.when(jnp.logical_not(first))
                def _():
                    h_taps()

            total = None
            for k in range(TAPS):
                term = dot(w_ref[k], cols[k], ((1,), (0,)))
                total = term if total is None else total + term
            for t in range(tiles):
                piece = total[:, t * pixels : (t + 1) * pixels]
                hout[t] = (hin[t].astype(jnp.float32) + piece).astype(jnp.bfloat16)
            h_line().start()

        @pl.when(first)
        def _():
            for j in range(PLANE):
                take_act(j)

        @pl.when(jnp.logical_not(last))
        def _():
            copy(gout, gin, line_send.at[1], line_recv.at[1], (pos + 1, me)).wait_recv()
            g_spread(gin)

        if sections > 2:

            @pl.when(jnp.logical_not(first) & jnp.logical_not(last))
            def _():
                g_taps()
                find_back()

        @pl.when(jnp.logical_not(first))
        def _():
            for t in range(tiles):
                value = hin[t].astype(jnp.float32)
                sig = jax.nn.sigmoid(value)
                slope = sig * (1.0 + value * (1.0 - sig))
                gout[t] = (gin[t].astype(jnp.float32) + slope * back[t]).astype(jnp.bfloat16)
            g_line().start()

    def gradient(j):
        return dot(stacks[j], acts[j], ((1,), (1,)))

    full = TAPS * rows
    wide = channels // LANES
    rest = channels - wide * LANES
    fits = LANES // rest
    tail = wide * full
    steady = TAPS // fits

    def place(k):
        if k < steady * fits:
            return tail + (k % steady) * rows, (k // steady) * rest
        return tail + (steady + k - steady * fits) * rows, 0

    def add_in(value, fresh):
        def put(start, piece):
            size = piece.shape[0]
            if fresh:
                acc[start : start + size, :] = piece
            else:
                acc[start : start + size, :] += piece

        for c in range(wide):
            put(c * full, value[:, c * LANES : (c + 1) * LANES])
        edge = value[:, wide * LANES :]
        span_rows = steady * rows
        sides = [edge[n * span_rows : (n + 1) * span_rows] for n in range(fits)]
        put(tail, jnp.concatenate(sides, axis=1))
        left = edge[fits * span_rows :]
        if left.shape[0]:
            put(tail + span_rows, jnp.concatenate([left] * fits, axis=1))

    used = tail + (steady + TAPS - steady * fits) * rows
    if groups * chunk > used:
        acc[used:, :] = jnp.zeros((groups * chunk - used, LANES), jnp.float32)
    @pl.when(last)
    def _():
        for j in range(PLANE):
            take_stack(j)

    for j in range(PLANE):
        if sections > 1:

            @pl.when(jnp.logical_not(first))
            def _():
                take_act(j)

        else:
            take_act(j)

        @pl.when(jnp.logical_not(last))
        def _():
            take_stack(j)

        add_in(gradient(j), j == 0)

    halves = [(0, (units + 1) // 2 * 16), ((units + 1) // 2 * 16, units // 2 * 16)]
    sides = [-1, 1]

    def span(index):
        return pl.ds(pl.multiple_of(index * chunk, 16), chunk)

    def toward(side, dest):
        return group < dest if side == 0 else group > dest

    def fed(side):
        return group > 0 if side == 0 else group < groups - 1

    def part_copy(side, dest, half):
        start, size = halves[half]
        where = pl.ds(start, size)
        device = (pos, (group - sides[side]) * PLANE + quarter)
        return copy(
            send_part.at[side, dest, where, :], got_part.at[side, dest, where, :],
            part_send.at[side, dest, half], part_recv.at[side, dest, half], device,
        )

    def part_wait(side, dest, half):
        start, size = halves[half]
        ref = got_part.at[side, dest, pl.ds(start, size), :]
        device = (pos, (group + sides[side]) * PLANE + quarter)
        copy(ref, ref, part_send.at[0, 0, 0], part_recv.at[side, dest, half], device).wait_recv()

    def hand_on(side, dest, half):
        start, size = halves[half]
        where = slice(start, start + size)
        rows_at = slice(dest * chunk + start, dest * chunk + start + size)

        @pl.when(toward(side, dest) & fed(side))
        def _():
            part_wait(side, dest, half)
            both = acc[rows_at, :] + got_part[side, dest, where, :].astype(jnp.float32)
            send_part[side, dest, where, :] = both.astype(jnp.bfloat16)

        @pl.when(toward(side, dest) & jnp.logical_not(fed(side)))
        def _():
            send_part[side, dest, where, :] = acc[rows_at, :].astype(jnp.bfloat16)

        @pl.when(toward(side, dest))
        def _():
            part_copy(side, dest, half).start()

    routes = [
        (side, groups - 1 - e if side == 0 else e, half)
        for e in range(groups - 1)
        for half in range(2)
        for side in range(2)
    ]
    for route in routes:
        hand_on(*route)
    for side in range(2):

        @pl.when(fed(side))
        def _():
            for half in range(2):
                part_wait(side, group, half)
            acc[span(group), :] += got_part[side, group].astype(jnp.float32)

    gathered[quarter, span(group), :] = acc[span(group), :].astype(jnp.bfloat16)

    def block(source, part):
        return gathered.at[source, span(part), :]


    def side_part(s, side):
        part = group + sides[side] * s
        return part, (part >= 0) & (part < groups)

    def side_open(side):
        other = group - sides[side]
        return (other >= 0) & (other < groups)

    def chain_copy(s, side):
        part = side_part(s, side)[0]
        ref = block(quarter, part)
        device = (pos, (group - sides[side]) * PLANE + quarter)
        return copy(ref, ref, z_send.at[side, s], all_recv.at[quarter, part], device)

    def near(part, j):
        ref = block(quarter, part)
        return copy(ref, ref, near_send.at[j - 1, part], all_recv.at[quarter, part], mate(j)[1])

    def half_block(source, part, half):
        start, size = halves[half]
        return gathered.at[source, pl.ds(pl.multiple_of(part * chunk + start, 16), size), :]

    def far(part, half):
        ref = half_block(mate(half + 1)[0], part, half)
        return copy(ref, ref, far_send.at[half, part], diag_recv.at[half, part], mate(2 - half)[1])

    def arrive(source, part):
        ref = block(source, part)
        copy(ref, ref, z_send.at[0, 0], all_recv.at[source, part], mate(1)[1]).wait_recv()

    def arrive_diag(part, half):
        ref = half_block(mate(3)[0], part, half)
        copy(ref, ref, far_send.at[half, part], diag_recv.at[half, part], mate(1)[1]).wait_recv()

    def near_both(part):
        near(part, 1).start()
        near(part, 2).start()

    def relay(part):
        for half in range(2):
            arrive(mate(half + 1)[0], part)
            far(part, half).start()

    for s in range(groups):
        for side in range(2):
            part, valid = side_part(s, side)
            if s:

                @pl.when(valid)
                def _():
                    arrive(quarter, part)

            @pl.when(valid & side_open(side))
            def _():
                chain_copy(s, side).start()

            if s == 0:
                if side == 1:
                    near_both(group)
                continue

            @pl.when(valid)
            def _():
                near_both(part)

        if s == 1:
            relay(group)
        elif s > 1:
            for side in range(2):
                part, valid = side_part(s - 1, side)

                @pl.when(valid)
                def _():
                    relay(part)

    if groups == 1:
        relay(group)
    else:
        for side in range(2):
            part, valid = side_part(groups - 1, side)

            @pl.when(valid)
            def _():
                relay(part)

    def update(source):
        where = pl.ds(pl.multiple_of(source * rows, 16), rows)
        for k in range(TAPS):
            pieces = [(c * full + k * rows, 0, c * LANES, LANES) for c in range(wide)]
            pieces.append(place(k) + (wide * LANES, rest))
            for start, lane, column_at, width in pieces:
                grad = gathered[source, start : start + rows, lane : lane + width].astype(jnp.float32)
                cols = slice(column_at, column_at + width)
                new_m = momentum_rate * new_m_ref[k, where, cols] + grad
                new_m_ref[k, where, cols] = new_m
                old = w_ref[k, where, cols].astype(jnp.float32)
                new_w_ref[k, where, cols] = (old - learn_rate * new_m).astype(jnp.bfloat16)

    loads[3].wait()
    update(quarter)
    update(mate(1)[0])
    update(mate(2)[0])
    for part in range(groups):
        arrive_diag(part, 0)
        arrive_diag(part, 1)
    update(mate(3)[0])
    for j in range(1, PLANE):
        h_copy(hin, j).wait_send()
        g_copy(gin, j).wait_send()
    for side, dest, half in routes:

        @pl.when(toward(side, dest))
        def _():
            part_copy(side, dest, half).wait_send()

    for part in range(groups):
        for n in range(2):
            near(part, n + 1).wait_send()
            far(part, n).wait_send()
    for s in range(groups):
        for side in range(2):

            @pl.when(side_part(s, side)[1] & side_open(side))
            def _():
                chain_copy(s, side).wait_send()

    if sections > 1:

        @pl.when(jnp.logical_not(last))
        def _():
            h_line().wait_send()

        @pl.when(jnp.logical_not(first))
        def _():
            g_line().wait_send()


def shards(sections, count, inputs, out_grad, weights, momentum):
    channels, pixels = inputs.shape[2:]
    x = inputs.reshape((-1, channels, pixels))
    y = out_grad.reshape((-1, channels, pixels))
    tiles = x.shape[0]
    w = jnp.transpose(weights[0], (1, 0, 2))
    m = jnp.transpose(momentum[0], (1, 0, 2))
    groups = count // PLANE
    rows = channels // PLANE
    wide, rest = divmod(channels, LANES)
    fits = LANES // rest
    spare = TAPS // fits + TAPS % fits
    units = -(-((wide * TAPS + spare) * rows // 16) // groups)
    chunk = units * 16
    height = groups * chunk
    bf16, f32 = jnp.bfloat16, jnp.float32
    vmem = pl.BlockSpec(memory_space=pltpu.VMEM)
    dma = pltpu.SemaphoreType.DMA
    hbm = pl.BlockSpec(memory_space=pltpu.HBM)
    new_w, new_m = pl.pallas_call(
        functools.partial(step_kernel, sections, count, units),
        out_shape=(
            jax.ShapeDtypeStruct(w.shape, bf16),
            jax.ShapeDtypeStruct(w.shape, f32),
        ),
        in_specs=[hbm] * 4,
        out_specs=(vmem, vmem),
        scratch_shapes=[
            pltpu.VMEM((tiles, channels, pixels), bf16),
            pltpu.VMEM((tiles, channels, pixels), bf16),
            pltpu.VMEM(w.shape, bf16),
            pltpu.VMEM((tiles, channels, pixels), bf16),
            pltpu.VMEM((tiles, channels, pixels), bf16),
            pltpu.VMEM((tiles, channels, pixels), bf16),
            pltpu.VMEM((tiles, channels, pixels), bf16),
            pltpu.VMEM((tiles, channels, pixels), f32),
            pltpu.VMEM((PLANE, tiles, channels, pixels), bf16),
            pltpu.VMEM((PLANE, tiles, rows, pixels), bf16),
            pltpu.VMEM((TAPS, channels, tiles * pixels), bf16),
            pltpu.VMEM((PLANE, channels, tiles * pixels), bf16),
            pltpu.VMEM((PLANE, TAPS * rows, tiles * pixels), bf16),
            pltpu.VMEM((height, LANES), f32),
            pltpu.VMEM((2, groups, chunk, LANES), bf16),
            pltpu.VMEM((2, groups, chunk, LANES), bf16),
            pltpu.VMEM((PLANE, height, LANES), bf16),
            dma((2,)), dma((2,)), dma((PLANE,)), dma((PLANE,)), dma((PLANE,)), dma((PLANE,)),
            dma((2, groups, 2)), dma((2, groups, 2)), dma((2, groups)), dma((PLANE, groups)),
            dma((2, groups)), dma((2, groups)), dma((2, groups)), dma((4,)),
        ],
        compiler_params=pltpu.CompilerParams(
            collective_id=0, has_side_effects=True, vmem_limit_bytes=44 * 1024 * 1024
        ),
    )(*[pltpu.with_memory_space_constraint(v, pltpu.HBM) for v in (x, y, w, m)])
    return jnp.transpose(new_w, (1, 0, 2))[None], jnp.transpose(new_m, (1, 0, 2))[None]


def solution(mesh):
    in_specs = (
        P(None, "dp", None, None),
        P(None, "dp", None, None),
        P("section", None, None, None),
        P("section", None, None, None),
    )
    out_specs = (P("section", None, None, None), P("section", None, None, None))
    body = functools.partial(shards, mesh.shape["section"], mesh.shape["dp"])
    return jax.shard_map(body, mesh=mesh, in_specs=in_specs, out_specs=out_specs, check_vma=False)
```
